32 devices in a mesh: prow: 4 (over x, core), pcol: 8 (over z, y).
Axes of the slice: x: 2, y: 2, z: 4, core: 2. Of those that a mesh axis runs over, the one named last changes fastest.
Arguments:
- b_leaf: bfloat16 [64, 256, 256], P('pcol', 'prow'), may hold values from -6 to 6
- dinv_leaf: bfloat16 [64, 256, 256], P('pcol'), as said below
- b_sep: bfloat16 [32, 256, 256], P('prow', 'pcol'), may hold values from -6 to 6
- dinv_sep: bfloat16 [32, 256, 256], P('prow'), as said below
- coupling: bfloat16 [32, 64, 256, 256], P('prow', 'pcol'), may hold values from -0.0625 to 0.0625
- pattern: int32 [32, 64], P('prow', 'pcol'), may hold values 0 or 1
Outputs:
- x_leaf: float32 [64, 256, 256], P('pcol', 'prow')
- x_sep: float32 [32, 256, 256], P('prow', 'pcol')
The draws below stay inside these ranges and needn't reach their ends.
Inputs may be any that keep to these rules, and one draw needn't show every extreme that they name: pattern holds only 0 and 1. dinv_leaf is a full matrix for every supernode. dinv_sep is a full matrix for every supernode.
All inputs are finite; a program needn't handle non-finite values. No bound on the sum of `pattern` on one device may be relied on, other than what follows from the above.
Results may differ from the reference program's by a relative error of at most 0.0048.
Values may be sent and summed in bfloat16 or wider, within the bound.
A program may use at most 64 MiB of HBM per device.

```python
import math
import jax
import jax.numpy as jnp
from jax import lax

BS = 256
R = 256
NL = 64
NS = 32


def dominant_blocks(key, count):
    first, second = jax.random.split(key)
    diagonal = jax.random.uniform(first, (count, BS), jnp.float32, 0.6, 1.6)
    noise = jax.random.normal(second, (count, BS, BS), jnp.float32) * (0.5 / math.sqrt(BS))
    eye_block = jnp.eye(BS, dtype=jnp.float32)
    return (eye_block[None, :, :] * diagonal[:, :, None] + noise).astype(jnp.bfloat16)


def draw_dinv_leaf(key, part):
    return dominant_blocks(jax.random.fold_in(key, 11), NL)


def draw_dinv_sep(key, part):
    return dominant_blocks(jax.random.fold_in(key, 23), NS)


def touch_ends(values, own_key, smallest, high):
    longest = values.shape.index(max(values.shape))
    spots = []
    for shift in (0, 1):
        where = [jax.random.randint(jax.random.fold_in(own_key, axis), (), 0, length) for axis, length in enumerate(values.shape)]
        where[longest] = (where[longest] + shift) % values.shape[longest]
        spots.append(tuple(where))
    return values.at[spots[0]].set(smallest).at[spots[1]].set(high)


def shard_levels(rng, shape, cuts, smallest, top_value):
    def one(dim, shards_of):
        heights = jax.random.uniform(jax.random.fold_in(jax.random.fold_in(rng, 6), dim), (shards_of,), jnp.float32, smallest / len(cuts), top_value / len(cuts))
        return jnp.repeat(jnp.exp(heights), shape[dim] // shards_of).reshape((-1,) + (1,) * (len(shape) - dim - 1))

    level = one(*cuts[0])
    for cut in cuts[1:]:
        level = level * one(*cut)
    return level


def centred(own_key, extent, scale, reach, pieces=(), kind=jnp.bfloat16):
    drawn = jax.random.normal(own_key, extent, jnp.float32) * scale
    if len(pieces) > 0:
        drawn = shard_levels(own_key, extent, pieces, -0.22, 0.18) * drawn
    return jnp.clip(drawn, min=-reach, max=reach).astype(kind)


def setup_inputs(seed: int = 0) -> dict:
    seeds = jax.random.split(jax.random.key(seed), 7)
    b_leaf = centred(seeds[0], (NL, R, BS), 1.0, 6.0, ((0, 8), (1, 4)))
    dinv_leaf = draw_dinv_leaf(jax.random.fold_in(seeds[6], 71), 0)
    b_sep = centred(seeds[2], (NS, R, BS), 1.0, 6.0, ((0, 4), (1, 8)))
    dinv_sep = draw_dinv_sep(jax.random.fold_in(seeds[6], 71), 0)
    coupling = centred(seeds[4], (NS, NL, BS, BS), (BS * NL // 2) ** -0.5, 0.0625, ((0, 4), (1, 8)))
    pattern = touch_ends((jax.random.randint(seeds[5], (NS, NL), 0, 2) < 1).astype(jnp.int32), jax.random.fold_in(seeds[5], 1), 0, 1)
    return {"b_leaf": b_leaf, "dinv_leaf": dinv_leaf, "b_sep": b_sep, "dinv_sep": dinv_sep, "coupling": coupling, "pattern": pattern}


def reference(b_leaf, dinv_leaf, b_sep, dinv_sep, coupling, pattern):
    f32 = jnp.float32
    solved = jnp.einsum("lrk,ljk->lrj", b_leaf.astype(f32), dinv_leaf.astype(f32)).astype(jnp.bfloat16)
    solved = lax.optimization_barrier(solved)
    solved_f = solved.astype(f32)

    def forward(item):
        block, mask_row = item
        masked = block.astype(f32) * mask_row.astype(f32)[:, None, None]
        return jnp.einsum("lrk,ljk->rj", solved_f, masked)

    update = lax.map(forward, (coupling, pattern))
    reduced = b_sep.astype(f32) - update
    reduced_b = lax.optimization_barrier(reduced.astype(jnp.bfloat16))
    forward_sep = jnp.einsum("srk,sjk->srj", reduced_b.astype(f32), dinv_sep.astype(f32)).astype(jnp.bfloat16)
    forward_sep = lax.optimization_barrier(forward_sep)
    x_sep = jnp.einsum("srk,skj->srj", forward_sep.astype(f32), dinv_sep.astype(f32))
    x_sep_b = lax.optimization_barrier(x_sep.astype(jnp.bfloat16))

    def backward(carry, item):
        block, mask_row, row_values = item
        masked = block.astype(f32) * mask_row.astype(f32)[:, None, None]
        return carry + jnp.einsum("rj,ljk->lrk", row_values.astype(f32), masked), None

    start = jnp.zeros(solved.shape, f32)
    total, _ = lax.scan(backward, start, (coupling, pattern, x_sep_b))
    corrected = solved_f - total
    corrected_b = lax.optimization_barrier(corrected.astype(jnp.bfloat16))
    x_leaf = jnp.einsum("lrk,lkj->lrj", corrected_b.astype(f32), dinv_leaf.astype(f32))
    return x_leaf, x_sep
```

```python
import functools

import jax
import jax.numpy as jnp
from jax import lax
from jax.experimental import pallas as pl
from jax.experimental.pallas import tpu as pltpu
from jax.sharding import PartitionSpec as P

BF = jnp.bfloat16
F32 = jnp.float32
MESH = pl.DeviceIdType.MESH


def factors(pc):
    ny = 1
    while 2 * ny * ny <= pc // 2:
        ny *= 2
    return pc // ny, ny


def dot_t(a, b):
    return lax.dot_general(a, b, (((1,), (1,)), ((), ())), preferred_element_type=F32)


def dot_n(a, b):
    return lax.dot_general(a, b, (((1,), (0,)), ((), ())), preferred_element_type=F32)


def rows_of(v):
    n, r, w = v.shape
    if r % 16:
        return v.astype(F32).reshape(n * r, w).astype(v.dtype)
    return v.reshape(n * r, w)


def kernel(dims, b_leaf, dinv_leaf, b_sep, dinv_sep, coupling, pattern, x_leaf, x_sep,
           c_v, dl_v, ds_v, bs_v, bl_all, solved, pbuf, rec_y, zbuf, rec_z, xg, back,
           ebuf, rec_e1, e2buf, rec_e2, loc_sem, c_sem,
           a_s, a_r, as_s, as_r, y_s, y_r, z_s, z_r, d_s, d_r, f_s, f_r, e_s, e_r, g_s, g_r):
    nx, nz, ny, ls, ss, rl, rs, step = dims
    p, q = lax.axis_index("prow"), lax.axis_index("pcol")
    x, core = p // 2, p % 2
    z, y = q // ny, q % ny
    sib = (x * 2 + (1 - core), q)
    nch = ss // step
    lch = ls // step

    def at_x(d):
        return lax.rem(x + d + nx, nx)

    def at_y(d):
        return lax.rem(y + d + ny, ny)

    def at_z(d):
        return lax.rem(z + d + nz, nz)

    def dev_x(d):
        return (at_x(d) * 2 + core, q)

    def dev_y(d):
        return (p, z * ny + at_y(d))

    def dev_z(d):
        return (p, at_z(d) * ny + y)

    def remote(src, dst, s_sem, r_sem, dev):
        return pltpu.make_async_remote_copy(
            src_ref=src, dst_ref=dst, send_sem=s_sem, recv_sem=r_sem,
            device_id=dev, device_id_type=MESH)

    own = pltpu.make_async_copy(b_leaf, bl_all.at[p], loc_sem.at[0])
    own.start()
    locs = [pltpu.make_async_copy(dinv_leaf, dl_v, loc_sem.at[1]),
            pltpu.make_async_copy(dinv_sep, ds_v, loc_sem.at[2]),
            pltpu.make_async_copy(b_sep, bs_v, loc_sem.at[3])]
    cps = [pltpu.make_async_copy(coupling.at[s], c_v.at[s], c_sem.at[s]) for s in range(ss)]

    barrier = pltpu.get_barrier_semaphore()
    peers = ([dev_x(d) for d in range(1, nx)] + [sib] + [dev_y(d) for d in range(1, ny)]
             + [dev_z(d) for d in range(1, nz)])
    for dev in peers:
        pl.semaphore_signal(barrier, inc=1, device_id=dev, device_id_type=MESH)
    pl.semaphore_wait(barrier, len(peers))

    sends = []

    a_copies = {}
    as_copies = {}
    for t in range(lch):
        part = pl.ds(t * step, step)
        for d in range(1, nx):
            cp = remote(b_leaf.at[part], bl_all.at[p, part], a_s.at[d - 1, t], a_r.at[d - 1, t], dev_x(d))
            cp.start()
            a_copies[d, t] = cp
        cp = remote(b_leaf.at[part], bl_all.at[p, part], as_s.at[0, t], as_r.at[0, t], sib)
        cp.start()
        as_copies[0, t] = cp
    for cp in locs + cps:
        cp.start()

    def mask_row(s):
        cps[s].wait()

        @pl.loop(0, ls)
        def _(l):
            c_v[s, l] = c_v[s, l] * pattern[s, l].astype(F32).astype(BF)

    def forward_a(t):
        part = pl.ds(t * step, step)
        for d in range(1, nx):
            a_copies[d, t].wait_recv()
            src = bl_all.at[at_x(-d) * 2 + core, part]
            cp = remote(src, src, as_s.at[d, t], as_r.at[d, t], sib)
            cp.start()
            as_copies[d, t] = cp

    def solve_leaf(t):
        for d in range(nx):
            as_copies[d, t].wait_recv()

        @pl.loop(t * step, (t + 1) * step)
        def _(l):
            solved[l] = dot_t(rows_of(bl_all[:, l]), dl_v[l]).astype(BF)

    per = ss // lch
    for t in range(lch):
        for s in range(t * per, (t + 1) * per):
            mask_row(s)
        forward_a(t)
    own.wait()
    locs[0].wait()
    for t in range(lch):
        solve_leaf(t)
    locs[1].wait()
    locs[2].wait()

    y_copies, z_copies, d_copies, f_copies = {}, {}, {}, {}

    def partial(t):
        @pl.loop(t * step, (t + 1) * step)
        def _(s):
            total = dot_t(solved[0], c_v[s, 0])
            for l in range(1, ls):
                total += dot_t(solved[l], c_v[s, l])
            total = total.reshape(nz, ny, rs, total.shape[-1])
            for j in range(ny):
                pbuf[j, s] = total[:, j].astype(BF)
        part = pl.ds(t * step, step)
        for d in range(1, ny):
            cp = remote(pbuf.at[at_y(d), part], rec_y.at[d - 1, part],
                        y_s.at[d - 1, t], y_r.at[d - 1, t], dev_y(d))
            cp.start()
            y_copies[d, t] = cp

    def sum_y(t):
        for d in range(1, ny):
            y_copies[d, t].wait_recv()

        @pl.loop(t * step, (t + 1) * step)
        def _(s):
            total = pbuf[y, s].astype(F32)
            for d in range(1, ny):
                total += rec_y[d - 1, s].astype(F32)
            total = total.astype(BF)
            for j in range(nz):
                zbuf[j, s] = total[j]
        part = pl.ds(t * step, step)
        for d in range(1, nz):
            cp = remote(zbuf.at[at_z(d), part], rec_z.at[d - 1, part],
                        z_s.at[d - 1, t], z_r.at[d - 1, t], dev_z(d))
            cp.start()
            z_copies[d, t] = cp

    def solve_sep(t):
        for d in range(1, nz):
            z_copies[d, t].wait_recv()

        @pl.loop(t * step, (t + 1) * step)
        def _(s):
            total = zbuf[z, s].astype(F32)
            for d in range(1, nz):
                total += rec_z[d - 1, s].astype(F32)
            reduced = (bs_v[s].astype(F32) - total).astype(BF)
            fwd = dot_t(reduced, ds_v[s]).astype(BF)
            sol = dot_n(fwd, ds_v[s])
            x_sep[s] = sol
            xg[q, s] = sol.astype(BF)
        part = pl.ds(t * step, step)
        src = xg.at[q, part]
        for d in range(1, nz):
            cp = remote(src, src, d_s.at[d - 1, t], d_r.at[d - 1, t], dev_z(d))
            cp.start()
            d_copies[d, t] = cp
        for d in range(1, ny):
            cp = remote(src, src, f_s.at[d - 1, 0, t], f_r.at[d - 1, 0, t], dev_y(d))
            cp.start()
            f_copies[d, 0, t] = cp

    def forward_d(t):
        part = pl.ds(t * step, step)
        for e in range(1, nz):
            d_copies[e, t].wait_recv()
            src = xg.at[at_z(-e) * ny + y, part]
            for d in range(1, ny):
                cp = remote(src, src, f_s.at[d - 1, e, t], f_r.at[d - 1, e, t], dev_y(d))
                cp.start()
                f_copies[d, e, t] = cp

    def back_mm(t):
        for e in range(nz):
            for d in range(1, ny):
                f_copies[d, e, t].wait_recv()
        vals = [rows_of(xg[:, t * step + i]) for i in range(step)]

        @pl.loop(0, ls)
        def _(l):
            total = dot_n(vals[0], c_v[t * step, l])
            for i in range(1, step):
                total += dot_n(vals[i], c_v[t * step + i, l])
            if t == 0:
                back[l] = total
            else:
                back[l] += total

    stages = [(partial, 0), (sum_y, 2), (solve_sep, 4), (forward_d, 6), (back_mm, 8)]
    for i in range(nch + 9):
        for fn, lag in reversed(stages):
            if 0 <= i - lag < nch:
                fn(i - lag)

    e_copies, g_copies = {}, {}

    def split_e(t):
        @pl.loop(t * step, (t + 1) * step)
        def _(l):
            v = back[l].reshape(nx, 2, rl, back.shape[-1])
            ebuf[0, l] = v[:, 0].astype(BF)
            ebuf[1, l] = v[:, 1].astype(BF)
        part = pl.ds(t * step, step)
        cp = remote(ebuf.at[1 - core, part], rec_e1.at[part], e_s.at[t], e_r.at[t], sib)
        cp.start()
        e_copies[t] = cp

    def sum_e(t):
        e_copies[t].wait_recv()

        @pl.loop(t * step, (t + 1) * step)
        def _(l):
            total = (ebuf[core, l].astype(F32) + rec_e1[l].astype(F32)).astype(BF)
            for j in range(nx):
                e2buf[j, l] = total[j]
        part = pl.ds(t * step, step)
        for d in range(1, nx):
            cp = remote(e2buf.at[at_x(d), part], rec_e2.at[d - 1, part],
                        g_s.at[d - 1, t], g_r.at[d - 1, t], dev_x(d))
            cp.start()
            g_copies[d, t] = cp

    def final(t):
        for d in range(1, nx):
            g_copies[d, t].wait_recv()

        @pl.loop(t * step, (t + 1) * step)
        def _(l):
            total = e2buf[x, l].astype(F32)
            for d in range(1, nx):
                total += rec_e2[d - 1, l].astype(F32)
            mine = solved[l, pl.ds(pl.multiple_of(p * rl, rl), rl), :].astype(F32)
            x_leaf[l] = dot_n((mine - total).astype(BF), dl_v[l])

    for fn in (split_e, sum_e, final):
        for t in range(lch):
            fn(t)

    for group in (a_copies, as_copies, y_copies, z_copies, d_copies, f_copies, e_copies, g_copies):
        for cp in group.values():
            cp.wait_send()


def shards(pr, pc, b_leaf, dinv_leaf, b_sep, dinv_sep, coupling, pattern):
    nx = pr // 2
    nz, ny = factors(pc)
    ss, ls, bs, _ = coupling.shape
    rl, rs = b_leaf.shape[1], b_sep.shape[1]
    step = 2
    nch, lch = ss // step, ls // step
    any_, vmem = pl.BlockSpec(memory_space=pl.ANY), pl.BlockSpec(memory_space=pltpu.VMEM)
    dma = pltpu.SemaphoreType.DMA
    mx, my, mz = max(nx - 1, 1), max(ny - 1, 1), max(nz - 1, 1)
    sems = []
    for shape in ((mx, lch), (nx, lch), (my, nch), (mz, nch), (mz, nch), (my, nz, nch), (lch,), (mx, lch)):
        sems += [dma(shape), dma(shape)]
    return pl.pallas_call(
        functools.partial(kernel, (nx, nz, ny, ls, ss, rl, rs, step)),
        out_shape=(jax.ShapeDtypeStruct(b_leaf.shape, F32), jax.ShapeDtypeStruct(b_sep.shape, F32)),
        in_specs=[any_] * 5 + [pl.BlockSpec(memory_space=pltpu.SMEM)],
        out_specs=(vmem, vmem),
        scratch_shapes=[
            pltpu.VMEM(coupling.shape, BF),
            pltpu.VMEM(dinv_leaf.shape, BF),
            pltpu.VMEM(dinv_sep.shape, BF),
            pltpu.VMEM(b_sep.shape, BF),
            pltpu.VMEM((pr, ls, rl, bs), BF),
            pltpu.VMEM((ls, pr * rl, bs), BF),
            pltpu.VMEM((ny, ss, nz, rs, bs), BF),
            pltpu.VMEM((my, ss, nz, rs, bs), BF),
            pltpu.VMEM((nz, ss, rs, bs), BF),
            pltpu.VMEM((mz, ss, rs, bs), BF),
            pltpu.VMEM((pc, ss, rs, bs), BF),
            pltpu.VMEM((ls, pr * rl, bs), F32),
            pltpu.VMEM((2, ls, nx, rl, bs), BF),
            pltpu.VMEM((ls, nx, rl, bs), BF),
            pltpu.VMEM((nx, ls, rl, bs), BF),
            pltpu.VMEM((mx, ls, rl, bs), BF),
            dma((4,)), dma((ss,)),
        ] + sems,
        compiler_params=pltpu.CompilerParams(
            collective_id=0, has_side_effects=True, vmem_limit_bytes=50 * 1024 * 1024),
    )(b_leaf, dinv_leaf, b_sep, dinv_sep, coupling, pattern)


def solution(mesh):
    pr, pc = mesh.shape["prow"], mesh.shape["pcol"]
    return jax.shard_map(
        functools.partial(shards, pr, pc),
        mesh=mesh,
        in_specs=(
            P("pcol", "prow", None),
            P("pcol", None, None),
            P("prow", "pcol", None),
            P("prow", None, None),
            P("prow", "pcol", None, None),
            P("prow", "pcol"),
        ),
        out_specs=(P("pcol", "prow", None), P("prow", "pcol", None)),
        check_vma=False,
    )
```

```python
import functools

import jax
import jax.numpy as jnp
from jax import lax
from jax.experimental import pallas as pl
from jax.experimental.pallas import tpu as pltpu
from jax.sharding import PartitionSpec as P

BF = jnp.bfloat16
F32 = jnp.float32
MESH = pl.DeviceIdType.MESH
LAGS = (2, 5, 8, 10)


def factors(pc):
    ny = 1
    while 2 * ny * ny <= pc // 2:
        ny *= 2
    return pc // ny, ny


def dot_t(a, b):
    return lax.dot_general(a, b, (((1,), (1,)), ((), ())), preferred_element_type=F32)


def dot_n(a, b):
    return lax.dot_general(a, b, (((1,), (0,)), ((), ())), preferred_element_type=F32)


def rows_of(v):
    r, w = v.shape[-2:]
    if r % 16:
        return v.astype(F32).reshape(-1, w).astype(v.dtype)
    return v.reshape(-1, w)


def kernel(dims, b_leaf, dinv_leaf, b_sep, dinv_sep, coupling, pattern, x_leaf, x_sep,
           c_v, dl_v, ds_v, bs_v, bl_all, solved, pbuf, rec_y, zbuf, rec_z, xg, back,
           ebuf, rec_e1, e2buf, rec_e2, own_sem, loc_sem, c_sem,
           a_s, a_r, as_s, as_r, y_s, y_r, z_s, z_r, d_s, d_r, f_s, f_r, e_s, e_r, g_s, g_r):
    nx, nz, ny, ls, ss, g, nh, rs, step = dims
    rl = g * rs
    p, q = lax.axis_index("prow"), lax.axis_index("pcol")
    x, core = p // 2, p % 2
    z, y = q // ny, q % ny
    sib = (x * 2 + (1 - core), q)
    nch = ss // step
    lch = ls // step

    def at_x(d):
        return lax.rem(x + d + nx, nx)

    def at_y(d):
        return lax.rem(y + d + ny, ny)

    def at_z(d):
        return lax.rem(z + d + nz, nz)

    def dev_x(d):
        return (at_x(d) * 2 + core, q)

    def dev_y(d):
        return (p, z * ny + at_y(d))

    def dev_z(d):
        return (p, at_z(d) * ny + y)

    def remote(src, dst, s_sem, r_sem, dev):
        return pltpu.make_async_remote_copy(
            src_ref=src, dst_ref=dst, send_sem=s_sem, recv_sem=r_sem,
            device_id=dev, device_id_type=MESH)

    own = [pltpu.make_async_copy(b_leaf.at[:, :, h], bl_all.at[h, p], own_sem.at[h]) for h in range(nh)]
    for cp in own:
        cp.start()
    locs = [pltpu.make_async_copy(dinv_leaf, dl_v, loc_sem.at[1]),
            pltpu.make_async_copy(dinv_sep, ds_v, loc_sem.at[2]),
            pltpu.make_async_copy(b_sep, bs_v, loc_sem.at[3])]
    cps = [pltpu.make_async_copy(coupling.at[s], c_v.at[s], c_sem.at[s]) for s in range(ss)]

    barrier = pltpu.get_barrier_semaphore()
    peers = ([dev_x(d) for d in range(1, nx)] + [sib] + [dev_y(d) for d in range(1, ny)]
             + [dev_z(d) for d in range(1, nz)])
    for dev in peers:
        pl.semaphore_signal(barrier, inc=1, device_id=dev, device_id_type=MESH)
    pl.semaphore_wait(barrier, len(peers))

    a_copies = {}
    as_copies = {}
    for h in range(nh):
        for t in range(lch):
            u = h * lch + t
            part = pl.ds(t * step, step)
            for d in range(1, nx):
                cp = remote(b_leaf.at[part, :, h], bl_all.at[h, p, part], a_s.at[d - 1, u], a_r.at[d - 1, u], dev_x(d))
                cp.start()
                a_copies[d, u] = cp
            cp = remote(b_leaf.at[part, :, h], bl_all.at[h, p, part], as_s.at[0, u], as_r.at[0, u], sib)
            cp.start()
            as_copies[0, u] = cp
    for cp in locs + cps:
        cp.start()

    def mask_row(s):
        cps[s].wait()

        @pl.loop(0, ls)
        def _(l):
            c_v[s, l] = c_v[s, l] * pattern[s, l].astype(F32).astype(BF)

    def forward_a(u):
        h, part = u // lch, pl.ds(u % lch * step, step)
        for d in range(1, nx):
            a_copies[d, u].wait_recv()
            src = bl_all.at[h, at_x(-d) * 2 + core, part]
            cp = remote(src, src, as_s.at[d, u], as_r.at[d, u], sib)
            cp.start()
            as_copies[d, u] = cp

    def solve_leaf(u):
        h, t = u // lch, u % lch
        for d in range(nx):
            as_copies[d, u].wait_recv()

        @pl.loop(t * step, (t + 1) * step)
        def _(l):
            solved[h, l] = dot_t(rows_of(bl_all[h, :, l]), dl_v[l]).astype(BF)

    y_copies, z_copies, d_copies, f_copies = {}, {}, {}, {}

    def partial(u):
        h, t = u // nch, u % nch

        @pl.loop(t * step, (t + 1) * step)
        def _(s):
            total = dot_t(solved[h, 0], c_v[s, 0])
            for l in range(1, ls):
                total += dot_t(solved[h, l], c_v[s, l])
            total = total.reshape(nz, ny, rs, total.shape[-1])
            for j in range(ny):
                pbuf[h, j, s] = total[:, j].astype(BF)
        part = pl.ds(t * step, step)
        for d in range(1, ny):
            cp = remote(pbuf.at[h, at_y(d), part], rec_y.at[h, d - 1, part],
                        y_s.at[d - 1, u], y_r.at[d - 1, u], dev_y(d))
            cp.start()
            y_copies[d, u] = cp

    def sum_y(u):
        h, t = u // nch, u % nch
        for d in range(1, ny):
            y_copies[d, u].wait_recv()

        @pl.loop(t * step, (t + 1) * step)
        def _(s):
            total = pbuf[h, y, s].astype(F32)
            for d in range(1, ny):
                total += rec_y[h, d - 1, s].astype(F32)
            total = total.astype(BF)
            for j in range(nz):
                zbuf[h, j, s] = total[j]
        part = pl.ds(t * step, step)
        for d in range(1, nz):
            cp = remote(zbuf.at[h, at_z(d), part], rec_z.at[h, d - 1, part],
                        z_s.at[d - 1, u], z_r.at[d - 1, u], dev_z(d))
            cp.start()
            z_copies[d, u] = cp

    def solve_sep(u):
        h, t = u // nch, u % nch
        for d in range(1, nz):
            z_copies[d, u].wait_recv()

        @pl.loop(t * step, (t + 1) * step)
        def _(s):
            total = zbuf[h, z, s].astype(F32)
            for d in range(1, nz):
                total += rec_z[h, d - 1, s].astype(F32)
            reduced = (bs_v[s, h].astype(F32) - total).astype(BF)
            fwd = dot_t(reduced, ds_v[s]).astype(BF)
            sol = dot_n(fwd, ds_v[s])
            x_sep[s, h] = sol
            xg[h, q, s] = sol.astype(BF)
        src = xg.at[h, q, pl.ds(t * step, step)]
        for d in range(1, nz):
            cp = remote(src, src, d_s.at[d - 1, u], d_r.at[d - 1, u], dev_z(d))
            cp.start()
            d_copies[d, u] = cp
        for d in range(1, ny):
            cp = remote(src, src, f_s.at[d - 1, 0, u], f_r.at[d - 1, 0, u], dev_y(d))
            cp.start()
            f_copies[d, 0, u] = cp

    def forward_d(u):
        h, part = u // nch, pl.ds(u % nch * step, step)
        for e in range(1, nz):
            d_copies[e, u].wait_recv()
            src = xg.at[h, at_z(-e) * ny + y, part]
            for d in range(1, ny):
                cp = remote(src, src, f_s.at[d - 1, e, u], f_r.at[d - 1, e, u], dev_y(d))
                cp.start()
                f_copies[d, e, u] = cp

    def back_mm(u):
        h, t = u // nch, u % nch
        for e in range(nz):
            for d in range(1, ny):
                f_copies[d, e, u].wait_recv()
        vals = [rows_of(xg[h, :, t * step + i]) for i in range(step)]

        @pl.loop(0, ls)
        def _(l):
            total = dot_n(vals[0], c_v[t * step, l])
            for i in range(1, step):
                total += dot_n(vals[i], c_v[t * step + i, l])
            if t == 0:
                back[h, l] = total
            else:
                back[h, l] += total

    e_copies, g_copies = {}, {}

    def split_e(u):
        h, t = u // lch, u % lch

        @pl.loop(t * step, (t + 1) * step)
        def _(l):
            v = back[h, l].reshape(nx, 2, rl, back.shape[-1])
            ebuf[h, 0, l] = v[:, 0].astype(BF)
            ebuf[h, 1, l] = v[:, 1].astype(BF)
        part = pl.ds(t * step, step)
        cp = remote(ebuf.at[h, 1 - core, part], rec_e1.at[h, part], e_s.at[u], e_r.at[u], sib)
        cp.start()
        e_copies[u] = cp

    def sum_e(u):
        h, t = u // lch, u % lch
        e_copies[u].wait_recv()

        @pl.loop(t * step, (t + 1) * step)
        def _(l):
            total = (ebuf[h, core, l].astype(F32) + rec_e1[h, l].astype(F32)).astype(BF)
            for j in range(nx):
                e2buf[h, j, l] = total[j]
        part = pl.ds(t * step, step)
        for d in range(1, nx):
            cp = remote(e2buf.at[h, at_x(d), part], rec_e2.at[h, d - 1, part],
                        g_s.at[d - 1, u], g_r.at[d - 1, u], dev_x(d))
            cp.start()
            g_copies[d, u] = cp

    def final(u):
        h, t = u // lch, u % lch
        for d in range(1, nx):
            g_copies[d, u].wait_recv()

        @pl.loop(t * step, (t + 1) * step)
        def _(l):
            total = e2buf[h, x, l].astype(F32)
            for d in range(1, nx):
                total += rec_e2[h, d - 1, l].astype(F32)
            mine = solved[h, l, pl.ds(pl.multiple_of(p * rl, rl), rl), :].astype(F32)
            sol = dot_n((mine - total).astype(BF), dl_v[l])
            x_leaf[l, :, h] = sol.reshape(g, rs, sol.shape[-1])

    per = ss // lch
    tasks = []
    for t in range(lch):
        tasks += [(mask_row, s) for s in range(t * per, (t + 1) * per)] + [(forward_a, t)]
    tasks += [(solve_leaf, t) for t in range(lch)]
    stages = [(partial, 0), (sum_y, LAGS[0]), (solve_sep, LAGS[1]), (forward_d, LAGS[2]), (back_mm, LAGS[3])]
    total_u = nh * nch
    for i in range(total_u + LAGS[3]):
        for fn, lag in reversed(stages):
            u = i - lag
            if not 0 <= u < total_u:
                continue
            h, t = u // nch, u % nch
            if fn is partial and t == 0 and h > 0:
                tasks += [(solve_leaf, h * lch + k) for k in range(lch)]
            tasks.append((fn, u))
            if fn is partial and t == nch // 2 and h + 1 < nh:
                tasks += [(forward_a, (h + 1) * lch + k) for k in range(lch)]
            if fn is back_mm:
                if h > 0 and t == nch // 2 - 1:
                    tasks += [(sum_e, (h - 1) * lch + k) for k in range(lch)]
                if t == nch - 1:
                    tasks += [(split_e, h * lch + k) for k in range(lch)]
                    if h > 0:
                        tasks += [(final, (h - 1) * lch + k) for k in range(lch)]
    tasks += [(fn, (nh - 1) * lch + k) for fn in (sum_e, final) for k in range(lch)]

    for k, (fn, u) in enumerate(tasks):
        if fn is solve_leaf and u % lch == 0:
            own[u // lch].wait()
            if u == 0:
                locs[0].wait()
        if fn is solve_sep and u == 0:
            locs[1].wait()
            locs[2].wait()
        fn(u)

    for group in (a_copies, as_copies, y_copies, z_copies, d_copies, f_copies, e_copies, g_copies):
        for cp in group.values():
            cp.wait_send()


def shards(pr, pc, b_leaf, dinv_leaf, b_sep, dinv_sep, coupling, pattern):
    nx = pr // 2
    nz, ny = factors(pc)
    ss, ls, bs, _ = coupling.shape
    g = pc // pr
    nh = 2 if b_sep.shape[1] >= 16 else 1
    rs = b_sep.shape[1] // nh
    rl = g * rs
    step = 2
    nch, lch = ss // step, ls // step
    nu, lu = nh * nch, nh * lch
    hbm, vmem = pl.BlockSpec(memory_space=pltpu.HBM), pl.BlockSpec(memory_space=pltpu.VMEM)
    dma = pltpu.SemaphoreType.DMA
    mx, my, mz = max(nx - 1, 1), max(ny - 1, 1), max(nz - 1, 1)
    sems = []
    for shape in ((mx, lu), (nx, lu), (my, nu), (mz, nu), (mz, nu), (my, nz, nu), (lu,), (mx, lu)):
        sems += [dma(shape), dma(shape)]
    x_leaf, x_sep = pl.pallas_call(
        functools.partial(kernel, (nx, nz, ny, ls, ss, g, nh, rs, step)),
        out_shape=(jax.ShapeDtypeStruct((ls, g, nh, rs, bs), F32), jax.ShapeDtypeStruct((ss, nh, rs, bs), F32)),
        in_specs=[hbm] * 5 + [pl.BlockSpec(memory_space=pltpu.SMEM)],
        out_specs=(vmem, vmem),
        scratch_shapes=[
            pltpu.VMEM(coupling.shape, BF),
            pltpu.VMEM(dinv_leaf.shape, BF),
            pltpu.VMEM(dinv_sep.shape, BF),
            pltpu.VMEM((ss, nh, rs, bs), BF),
            pltpu.VMEM((nh, pr, ls, g, rs, bs), BF),
            pltpu.VMEM((nh, ls, pr * rl, bs), BF),
            pltpu.VMEM((nh, ny, ss, nz, rs, bs), BF),
            pltpu.VMEM((nh, my, ss, nz, rs, bs), BF),
            pltpu.VMEM((nh, nz, ss, rs, bs), BF),
            pltpu.VMEM((nh, mz, ss, rs, bs), BF),
            pltpu.VMEM((nh, pc, ss, rs, bs), BF),
            pltpu.VMEM((nh, ls, pr * rl, bs), F32),
            pltpu.VMEM((nh, 2, ls, nx, rl, bs), BF),
            pltpu.VMEM((nh, ls, nx, rl, bs), BF),
            pltpu.VMEM((nh, nx, ls, rl, bs), BF),
            pltpu.VMEM((nh, mx, ls, rl, bs), BF),
            dma((nh,)), dma((4,)), dma((ss,)),
        ] + sems,
        compiler_params=pltpu.CompilerParams(
            collective_id=0, has_side_effects=True, vmem_limit_bytes=67043328),
    )(b_leaf.reshape(ls, g, nh, rs, bs), dinv_leaf, b_sep.reshape(ss, nh, rs, bs), dinv_sep, coupling, pattern)
    return x_leaf.reshape(b_leaf.shape), x_sep.reshape(b_sep.shape)


def solution(mesh):
    pr, pc = mesh.shape["prow"], mesh.shape["pcol"]
    return jax.shard_map(
        functools.partial(shards, pr, pc),
        mesh=mesh,
        in_specs=(
            P("pcol", "prow", None),
            P("pcol", None, None),
            P("prow", "pcol", None),
            P("prow", None, None),
            P("prow", "pcol", None, None),
            P("prow", "pcol"),
        ),
        out_specs=(P("pcol", "prow", None), P("prow", "pcol", None)),
        check_vma=False,
    )
```

```python
import functools

import jax
import jax.numpy as jnp
from jax import lax
from jax.experimental import pallas as pl
from jax.experimental.pallas import tpu as pltpu
from jax.sharding import PartitionSpec as P

BF = jnp.bfloat16
F32 = jnp.float32
MESH = pl.DeviceIdType.MESH
LAGS = (2, 4, 6, 8)


def factors(pc):
    ny = 1
    while 2 * ny * ny <= pc // 2:
        ny *= 2
    return pc // ny, ny


def dot_t(a, b):
    return lax.dot_general(a, b, (((1,), (1,)), ((), ())), preferred_element_type=F32)


def dot_n(a, b):
    return lax.dot_general(a, b, (((1,), (0,)), ((), ())), preferred_element_type=F32)


def rows_of(v):
    r, w = v.shape[-2:]
    if r % 16:
        return v.astype(F32).reshape(-1, w).astype(v.dtype)
    return v.reshape(-1, w)


def kernel(dims, b_leaf, dinv_leaf, b_sep, dinv_sep, coupling, pattern, x_leaf, x_sep,
           c_v, dl_v, ds_v, bs_v, bl_all, solved, pbuf, rec_y, zbuf, rec_z, xg, back,
           ebuf, rec_e1, e2buf, rec_e2, own_sem, loc_sem, c_sem,
           a_s, a_r, as_s, as_r, y_s, y_r, z_s, z_r, d_s, d_r, f_s, f_r, e_s, e_r, g_s, g_r):
    nx, nz, ny, ls, ss, g, nh, rs, step = dims
    rl = g * rs
    p, q = lax.axis_index("prow"), lax.axis_index("pcol")
    x, core = p // 2, p % 2
    z, y = q // ny, q % ny
    sib = (x * 2 + (1 - core), q)
    nch = ss // step
    lch = ls // step

    def at_x(d):
        return lax.rem(x + d + nx, nx)

    def at_y(d):
        return lax.rem(y + d + ny, ny)

    def at_z(d):
        return lax.rem(z + d + nz, nz)

    def dev_x(d):
        return (at_x(d) * 2 + core, q)

    def dev_y(d):
        return (p, z * ny + at_y(d))

    def dev_z(d):
        return (p, at_z(d) * ny + y)

    def remote(src, dst, s_sem, r_sem, dev):
        return pltpu.make_async_remote_copy(
            src_ref=src, dst_ref=dst, send_sem=s_sem, recv_sem=r_sem,
            device_id=dev, device_id_type=MESH)

    own = [pltpu.make_async_copy(b_leaf.at[:, :, h], bl_all.at[h, p], own_sem.at[h]) for h in range(nh)]
    for cp in own:
        cp.start()
    locs = [pltpu.make_async_copy(dinv_leaf, dl_v, loc_sem.at[1]),
            pltpu.make_async_copy(dinv_sep, ds_v, loc_sem.at[2]),
            pltpu.make_async_copy(b_sep, bs_v, loc_sem.at[3])]
    cps = [pltpu.make_async_copy(coupling.at[s], c_v.at[s], c_sem.at[s]) for s in range(ss)]

    barrier = pltpu.get_barrier_semaphore()
    peers = ([dev_x(d) for d in range(1, nx)] + [sib] + [dev_y(d) for d in range(1, ny)]
             + [dev_z(d) for d in range(1, nz)])
    for dev in peers:
        pl.semaphore_signal(barrier, inc=1, device_id=dev, device_id_type=MESH)
    pl.semaphore_wait(barrier, len(peers))

    a_copies = {}
    as_copies = {}
    for h in range(nh):
        for t in range(lch):
            u = h * lch + t
            part = pl.ds(t * step, step)
            for d in range(1, nx):
                cp = remote(b_leaf.at[part, :, h], bl_all.at[h, p, part], a_s.at[d - 1, u], a_r.at[d - 1, u], dev_x(d))
                cp.start()
                a_copies[d, u] = cp
            cp = remote(b_leaf.at[part, :, h], bl_all.at[h, p, part], as_s.at[0, u], as_r.at[0, u], sib)
            cp.start()
            as_copies[0, u] = cp
    for cp in locs + cps:
        cp.start()

    def mask_row(s):
        cps[s].wait()

        @pl.loop(0, ls)
        def _(l):
            c_v[s, l] = c_v[s, l] * pattern[s, l].astype(F32).astype(BF)

    def forward_a(u):
        h, part = u // lch, pl.ds(u % lch * step, step)
        for d in range(1, nx):
            a_copies[d, u].wait_recv()
            src = bl_all.at[h, at_x(-d) * 2 + core, part]
            cp = remote(src, src, as_s.at[d, u], as_r.at[d, u], sib)
            cp.start()
            as_copies[d, u] = cp

    def solve_leaf(u):
        h, t = u // lch, u % lch
        for d in range(nx):
            as_copies[d, u].wait_recv()

        @pl.loop(t * step, (t + 1) * step)
        def _(l):
            solved[h, l] = dot_t(rows_of(bl_all[h, :, l]), dl_v[l]).astype(BF)

    y_copies, z_copies, d_copies, f_copies = {}, {}, {}, {}

    def partial(u):
        h, t = u // nch, u % nch

        @pl.loop(t * step, (t + 1) * step)
        def _(s):
            total = dot_t(solved[h, 0], c_v[s, 0])
            for l in range(1, ls):
                total += dot_t(solved[h, l], c_v[s, l])
            total = total.reshape(nz, ny, rs, total.shape[-1])
            for j in range(ny):
                pbuf[h, j, s] = total[:, j].astype(BF)
        part = pl.ds(t * step, step)
        for d in range(1, ny):
            cp = remote(pbuf.at[h, at_y(d), part], rec_y.at[h, d - 1, part],
                        y_s.at[d - 1, u], y_r.at[d - 1, u], dev_y(d))
            cp.start()
            y_copies[d, u] = cp

    def sum_y(u):
        h, t = u // nch, u % nch
        for d in range(1, ny):
            y_copies[d, u].wait_recv()

        @pl.loop(t * step, (t + 1) * step)
        def _(s):
            total = pbuf[h, y, s].astype(F32)
            for d in range(1, ny):
                total += rec_y[h, d - 1, s].astype(F32)
            total = total.astype(BF)
            for j in range(nz):
                zbuf[h, j, s] = total[j]
        part = pl.ds(t * step, step)
        for d in range(1, nz):
            cp = remote(zbuf.at[h, at_z(d), part], rec_z.at[h, d - 1, part],
                        z_s.at[d - 1, u], z_r.at[d - 1, u], dev_z(d))
            cp.start()
            z_copies[d, u] = cp

    def solve_sep(u):
        h, t = u // nch, u % nch
        for d in range(1, nz):
            z_copies[d, u].wait_recv()

        @pl.loop(t * step, (t + 1) * step)
        def _(s):
            total = zbuf[h, z, s].astype(F32)
            for d in range(1, nz):
                total += rec_z[h, d - 1, s].astype(F32)
            reduced = (bs_v[s, h].astype(F32) - total).astype(BF)
            fwd = dot_t(reduced, ds_v[s]).astype(BF)
            sol = dot_n(fwd, ds_v[s])
            x_sep[s, h] = sol
            xg[h, q, s] = sol.astype(BF)
        src = xg.at[h, q, pl.ds(t * step, step)]
        for d in range(1, nz):
            cp = remote(src, src, d_s.at[d - 1, u], d_r.at[d - 1, u], dev_z(d))
            cp.start()
            d_copies[d, u] = cp
        for d in range(1, ny):
            cp = remote(src, src, f_s.at[d - 1, 0, u], f_r.at[d - 1, 0, u], dev_y(d))
            cp.start()
            f_copies[d, 0, u] = cp

    def forward_d(u):
        h, part = u // nch, pl.ds(u % nch * step, step)
        for e in range(1, nz):
            d_copies[e, u].wait_recv()
            src = xg.at[h, at_z(-e) * ny + y, part]
            for d in range(1, ny):
                cp = remote(src, src, f_s.at[d - 1, e, u], f_r.at[d - 1, e, u], dev_y(d))
                cp.start()
                f_copies[d, e, u] = cp

    def back_mm(u):
        h, t = u // nch, u % nch
        for e in range(nz):
            for d in range(1, ny):
                f_copies[d, e, u].wait_recv()
        vals = [rows_of(xg[h, :, t * step + i]) for i in range(step)]

        @pl.loop(0, ls)
        def _(l):
            total = dot_n(vals[0], c_v[t * step, l])
            for i in range(1, step):
                total += dot_n(vals[i], c_v[t * step + i, l])
            if t == 0:
                back[h, l] = total
            else:
                back[h, l] += total

    e_copies, g_copies = {}, {}

    def split_e(u):
        h, t = u // lch, u % lch

        @pl.loop(t * step, (t + 1) * step)
        def _(l):
            v = back[h, l].reshape(nx, 2, rl, back.shape[-1])
            ebuf[h, 0, l] = v[:, 0].astype(BF)
            ebuf[h, 1, l] = v[:, 1].astype(BF)
        part = pl.ds(t * step, step)
        cp = remote(ebuf.at[h, 1 - core, part], rec_e1.at[h, part], e_s.at[u], e_r.at[u], sib)
        cp.start()
        e_copies[u] = cp

    def sum_e(u):
        h, t = u // lch, u % lch
        e_copies[u].wait_recv()

        @pl.loop(t * step, (t + 1) * step)
        def _(l):
            total = (ebuf[h, core, l].astype(F32) + rec_e1[h, l].astype(F32)).astype(BF)
            for j in range(nx):
                e2buf[h, j, l] = total[j]
        part = pl.ds(t * step, step)
        for d in range(1, nx):
            cp = remote(e2buf.at[h, at_x(d), part], rec_e2.at[h, d - 1, part],
                        g_s.at[d - 1, u], g_r.at[d - 1, u], dev_x(d))
            cp.start()
            g_copies[d, u] = cp

    def final(u):
        h, t = u // lch, u % lch
        for d in range(1, nx):
            g_copies[d, u].wait_recv()

        @pl.loop(t * step, (t + 1) * step)
        def _(l):
            total = e2buf[h, x, l].astype(F32)
            for d in range(1, nx):
                total += rec_e2[h, d - 1, l].astype(F32)
            mine = solved[h, l, pl.ds(pl.multiple_of(p * rl, rl), rl), :].astype(F32)
            sol = dot_n((mine - total).astype(BF), dl_v[l])
            x_leaf[l, :, h] = sol.reshape(g, rs, sol.shape[-1])

    per = ss // lch
    tasks = []
    for t in range(lch):
        tasks += [(mask_row, s) for s in range(t * per, (t + 1) * per)] + [(forward_a, t)]
    tasks += [(solve_leaf, t) for t in range(lch)]
    stages = [(partial, 0), (sum_y, LAGS[0]), (solve_sep, LAGS[1]), (forward_d, LAGS[2]), (back_mm, LAGS[3])]
    total_u = nh * nch
    for i in range(total_u + LAGS[3]):
        for fn, lag in reversed(stages):
            u = i - lag
            if not 0 <= u < total_u:
                continue
            h, t = u // nch, u % nch
            if fn is partial and t == 0 and h > 0:
                tasks += [(solve_leaf, h * lch + k) for k in range(lch)]
            tasks.append((fn, u))
            if fn is partial and t == nch // 2 and h + 1 < nh:
                tasks += [(forward_a, (h + 1) * lch + k) for k in range(lch)]
            if fn is back_mm:
                if h > 0 and t == nch // 2 - 1:
                    tasks += [(sum_e, (h - 1) * lch + k) for k in range(lch)]
                if t == nch - 1:
                    tasks += [(split_e, h * lch + k) for k in range(lch)]
                    if h > 0:
                        tasks += [(final, (h - 1) * lch + k) for k in range(lch)]
    tasks += [(fn, (nh - 1) * lch + k) for fn in (sum_e, final) for k in range(lch)]

    for k, (fn, u) in enumerate(tasks):
        if fn is solve_leaf and u % lch == 0:
            own[u // lch].wait()
            if u == 0:
                locs[0].wait()
        if fn is solve_sep and u == 0:
            locs[1].wait()
            locs[2].wait()
        fn(u)

    for group in (a_copies, as_copies, y_copies, z_copies, d_copies, f_copies, e_copies, g_copies):
        for cp in group.values():
            cp.wait_send()


def shards(pr, pc, b_leaf, dinv_leaf, b_sep, dinv_sep, coupling, pattern):
    nx = pr // 2
    nz, ny = factors(pc)
    ss, ls, bs, _ = coupling.shape
    g = pc // pr
    nh = 1
    rs = b_sep.shape[1] // nh
    rl = g * rs
    step = 2
    nch, lch = ss // step, ls // step
    nu, lu = nh * nch, nh * lch
    hbm, vmem = pl.BlockSpec(memory_space=pltpu.HBM), pl.BlockSpec(memory_space=pltpu.VMEM)
    dma = pltpu.SemaphoreType.DMA
    mx, my, mz = max(nx - 1, 1), max(ny - 1, 1), max(nz - 1, 1)
    sems = []
    for shape in ((mx, lu), (nx, lu), (my, nu), (mz, nu), (mz, nu), (my, nz, nu), (lu,), (mx, lu)):
        sems += [dma(shape), dma(shape)]
    x_leaf, x_sep = pl.pallas_call(
        functools.partial(kernel, (nx, nz, ny, ls, ss, g, nh, rs, step)),
        out_shape=(jax.ShapeDtypeStruct((ls, g, nh, rs, bs), F32), jax.ShapeDtypeStruct((ss, nh, rs, bs), F32)),
        in_specs=[hbm] * 5 + [pl.BlockSpec(memory_space=pltpu.SMEM)],
        out_specs=(vmem, vmem),
        scratch_shapes=[
            pltpu.VMEM(coupling.shape, BF),
            pltpu.VMEM(dinv_leaf.shape, BF),
            pltpu.VMEM(dinv_sep.shape, BF),
            pltpu.VMEM((ss, nh, rs, bs), BF),
            pltpu.VMEM((nh, pr, ls, g, rs, bs), BF),
            pltpu.VMEM((nh, ls, pr * rl, bs), BF),
            pltpu.VMEM((nh, ny, ss, nz, rs, bs), BF),
            pltpu.VMEM((nh, my, ss, nz, rs, bs), BF),
            pltpu.VMEM((nh, nz, ss, rs, bs), BF),
            pltpu.VMEM((nh, mz, ss, rs, bs), BF),
            pltpu.VMEM((nh, pc, ss, rs, bs), BF),
            pltpu.VMEM((nh, ls, pr * rl, bs), F32),
            pltpu.VMEM((nh, 2, ls, nx, rl, bs), BF),
            pltpu.VMEM((nh, ls, nx, rl, bs), BF),
            pltpu.VMEM((nh, nx, ls, rl, bs), BF),
            pltpu.VMEM((nh, mx, ls, rl, bs), BF),
            dma((nh,)), dma((4,)), dma((ss,)),
        ] + sems,
        compiler_params=pltpu.CompilerParams(
            collective_id=0, has_side_effects=True, vmem_limit_bytes=67043328),
    )(b_leaf.reshape(ls, g, nh, rs, bs), dinv_leaf, b_sep.reshape(ss, nh, rs, bs), dinv_sep, coupling, pattern)
    return x_leaf.reshape(b_leaf.shape), x_sep.reshape(b_sep.shape)


def solution(mesh):
    pr, pc = mesh.shape["prow"], mesh.shape["pcol"]
    return jax.shard_map(
        functools.partial(shards, pr, pc),
        mesh=mesh,
        in_specs=(
            P("pcol", "prow", None),
            P("pcol", None, None),
            P("prow", "pcol", None),
            P("prow", None, None),
            P("prow", "pcol", None, None),
            P("prow", "pcol"),
        ),
        out_specs=(P("pcol", "prow", None), P("prow", "pcol", None)),
        check_vma=False,
    )
```
